32 devices in a mesh: cells: 8 (over z, x), cent: 4 (over y, core).
Axes of the slice: x: 2, y: 2, z: 4, core: 2. Of those that a mesh axis runs over, the one named last changes fastest.
Arguments:
- embed: float32 [64, 32768], P(None, 'cells'), may hold values from -240 to 240
- centroids: float32 [64, 2048], P(None, 'cent'), may hold values from -8 to 8
- cell_weight: float32 [32768], P('cells'), may hold values from 0.5 to 18, as said below
Outputs:
- new_centroids: float32 [64, 2048], P(None, 'cent')
- log_norms: float32 [32768], P('cells')
The draws below stay inside these ranges and needn't reach their ends.
Inputs may be any that keep to these rules, and one draw needn't show every extreme that they name: `cell_weight`: positive.
All inputs are finite; a program needn't handle non-finite values.
Results may differ from the reference program's by a relative error of at most 0.0003.
Values sent between devices are 32-bit elements; how exact they have to be, the bound alone decides.
A program may use at most 64 MiB of HBM per device.

```python
import jax
import jax.numpy as jnp
from jax import lax

COMPONENTS = 64
CENTROIDS = 2048
ROW_BLOCK = 512
ROUNDS = 2
CELLS = 32768


def shared_scales(key):
    return jnp.exp(jax.random.uniform(jax.random.fold_in(key, 7), (COMPONENTS,), jnp.float32, jnp.log(0.5), jnp.log(2.0)))


def centroid_table(key):
    scales = shared_scales(key)
    normal = jnp.clip(jax.random.normal(jax.random.fold_in(key, 11), (COMPONENTS, CENTROIDS), jnp.float32), -4.0, 4.0)
    table = 0.9 * normal * scales[:, None]
    return table


def batch_shift(key):
    scales = shared_scales(key)
    position = jnp.arange(CELLS).astype(jnp.float32) / (CELLS - 1)
    slope = jnp.clip(jax.random.normal(jax.random.fold_in(key, 23), (COMPONENTS,), jnp.float32), -3.0, 3.0)
    wave = jnp.clip(jax.random.normal(jax.random.fold_in(key, 29), (COMPONENTS,), jnp.float32), -3.0, 3.0)
    ripple = jnp.sin(3.0 * jnp.pi * position)
    return 0.3 * scales[:, None] * (slope[:, None] * (2.0 * position - 1.0)[None, :] + wave[:, None] * ripple[None, :])


def draw_centroids(key, part):
    return centroid_table(key)


def draw_embed(key, part):
    scales = shared_scales(key)
    table = centroid_table(key)
    member = jax.random.randint(jax.random.fold_in(key, 31), (CELLS,), 0, CENTROIDS)
    centers = jnp.take(table, member, axis=1)
    noise = 0.3 * jnp.clip(jax.random.normal(jax.random.fold_in(key, 13), (COMPONENTS, CELLS), jnp.float32), -4.0, 4.0)
    points = centers + batch_shift(key) + noise * scales[:, None]
    return points


def draw_cell_weight(key, part):
    position = jnp.arange(CELLS).astype(jnp.float32) / (CELLS - 1)
    base = jnp.exp(jax.random.uniform(jax.random.fold_in(key, 19), (CELLS,), jnp.float32, jnp.log(0.5), jnp.log(2.0)))
    return base * (1.0 + 2.0 * position)


def setup_inputs(seed: int = 0) -> dict:
    key_of = jax.random.split(jax.random.key(seed), 4)
    embed = draw_embed(jax.random.fold_in(key_of[3], 71), 0)
    centroids = draw_centroids(jax.random.fold_in(key_of[3], 71), 0)
    cell_weight = draw_cell_weight(jax.random.fold_in(key_of[3], 71), 0)
    return dict(embed=embed, centroids=centroids, cell_weight=cell_weight)


INV_TEMP = 0.125
PRIOR = 1.0


def reference(embed, centroids, cell_weight):
    features, cell_total = embed.shape
    blocks = cell_total // ROW_BLOCK
    current = centroids
    log_norms = None
    for round_id in range(ROUNDS):
        half_square = 0.5 * jnp.sum(current * current, axis=0)

        def one_block(totals, block_id, current=current, half_square=half_square):
            offset = (block_id * ROW_BLOCK).astype(jnp.int32)
            points = lax.dynamic_slice_in_dim(embed, offset, ROW_BLOCK, 1)
            weights = lax.dynamic_slice_in_dim(cell_weight, offset, ROW_BLOCK, 0)
            products = lax.dot_general(points, current, (((0,), (0,)), ((), ())), precision=lax.Precision.HIGHEST)
            logits = (products - half_square[None, :]) * INV_TEMP
            peak = jnp.max(logits, axis=1)
            lognorm = peak + jnp.log(jnp.sum(jnp.exp(logits - peak[:, None]), axis=1))
            shares = jnp.exp(logits - lognorm[:, None]) * weights[:, None]
            moment = totals[0] + jnp.dot(points, shares, precision=lax.Precision.HIGHEST)
            masses = totals[1] + jnp.sum(shares, axis=0)
            return (moment, masses), lognorm

        initial = (jnp.zeros((features, CENTROIDS), jnp.float32), jnp.zeros((CENTROIDS,), jnp.float32))
        (moment, masses), log_norms = lax.scan(one_block, initial, jnp.arange(blocks, dtype=jnp.int32))
        current = (moment + PRIOR * current) / (masses + PRIOR)[None, :]
    return current, log_norms.reshape(cell_total)
```

```python
import functools

import jax
import jax.numpy as jnp
from jax import lax
from jax.experimental import pallas as pl
from jax.experimental.pallas import tpu as pltpu
from jax.sharding import PartitionSpec as P

ROUNDS = 2
INV_TEMP = 0.125
PRIOR = 1.0
TILE = 256
TILE2 = 1024
LANES = 128
MESH = pl.DeviceIdType.MESH
BF16 = jnp.bfloat16
F32 = jnp.float32


def split(x):
    high = x.astype(BF16)
    return high, x - high.astype(F32)


def kernel(
    n_cells, n_cent,
    embed_ref, cent_ref, weight_ref,
    out_ref, norm_ref,
    points, table, high, low, logits, peaks, sums, factor,
    current, partial, norms, parts,
    norm_send, norm_recv, part_send, part_recv, new_send, new_recv,
):
    features, cells = embed_ref.shape
    width = cent_ref.shape[1]
    rows = cells // LANES
    chunk = width // n_cells
    me_cells = lax.axis_index("cells")
    me_cent = lax.axis_index("cent")

    barrier = pltpu.get_barrier_semaphore()
    for d in range(1, n_cent):
        pl.semaphore_signal(
            barrier, inc=1, device_id={"cent": lax.rem(me_cent + d, n_cent)}, device_id_type=MESH
        )
    for d in range(1, n_cells):
        pl.semaphore_signal(
            barrier, inc=1, device_id={"cells": lax.rem(me_cells + d, n_cells)}, device_id_type=MESH
        )

    def stack_points(i, _):
        cols = pl.ds(pl.multiple_of(i * TILE, TILE), TILE)
        e1, rest = split(embed_ref[:, cols])
        e2, rest = split(rest)
        e3 = rest.astype(BF16)
        for j, term in enumerate((e1, e1, e2, e2, e1, e3)):
            points[j * features:(j + 1) * features, cols] = term
        points[6 * features:, cols] = jnp.ones((2 * features, TILE), BF16)
        return 0

    lax.fori_loop(0, cells // TILE, stack_points, 0)

    lane = lax.broadcasted_iota(jnp.int32, (width, LANES), 1)
    left = lane < features
    start = cent_ref[...].T
    current[0] = jnp.concatenate([start, start], axis=1)

    for r in range(ROUNDS):
        both = current[r]
        half_square = 0.5 * jnp.sum(jnp.where(left, both * both, 0.0), axis=1, keepdims=True)
        c1, rest = split(both * INV_TEMP)
        c2, rest = split(rest)
        c3 = rest
        h1, rest = split(jnp.broadcast_to(half_square * -INV_TEMP, (width, LANES)))
        h2, h3 = split(rest)
        c1, c2, h1, h2 = (x.astype(F32) for x in (c1, c2, h1, h2))
        first = jnp.where(left, c1, c2).astype(BF16)
        table[:, 0:LANES] = first
        table[:, LANES:2 * LANES] = first
        table[:, 2 * LANES:3 * LANES] = jnp.where(left, c3, c1).astype(BF16)
        table[:, 3 * LANES:] = jnp.where(
            lane == 0, h1, jnp.where(lane == 1, h2, jnp.where(lane == 2, h3, 0.0))
        ).astype(BF16)

        def score(i, _):
            cols = pl.ds(pl.multiple_of(i * TILE, TILE), TILE)
            logits[...] = jnp.dot(table[...], points[:, cols], preferred_element_type=F32)
            step = 64
            peak = logits[0:step, :]
            for k in range(step, width, step):
                peak = jnp.maximum(peak, logits[k:k + step, :])
            peak = jnp.max(peak, axis=0, keepdims=True)
            total = jnp.zeros((step, TILE), F32)
            for k in range(0, width, step):
                p = jnp.exp(logits[k:k + step, :] - peak)
                total = total + p
                p1, p2 = split(p)
                high[k:k + step, cols] = p1
                low[k:k + step, cols] = p2.astype(BF16)
            total = jnp.sum(total, axis=0, keepdims=True)
            for j in range(TILE // LANES):
                row = pl.ds(i * (TILE // LANES) + j, 1)
                peaks[row, :] = peak[:, j * LANES:(j + 1) * LANES]
                sums[row, :] = total[:, j * LANES:(j + 1) * LANES]
            return 0

        lax.fori_loop(0, cells // TILE, score, 0)

        norms[r, me_cent] = peaks[...] + jnp.log(sums[...])
        if r == 0:
            pl.semaphore_wait(barrier, n_cent + n_cells - 2)
        copies = []
        for d in range(1, n_cent):
            copy = pltpu.make_async_remote_copy(
                src_ref=norms.at[r, me_cent],
                dst_ref=norms.at[r, me_cent],
                send_sem=norm_send.at[r, d],
                recv_sem=norm_recv.at[r, d],
                device_id={"cent": lax.rem(me_cent + d, n_cent)},
                device_id_type=MESH,
            )
            copy.start()
            copies.append(copy)
        for copy in copies:
            copy.wait()
        top = norms[r, 0]
        for d in range(1, n_cent):
            top = jnp.maximum(top, norms[r, d])
        total = jnp.zeros((rows, LANES), F32)
        for d in range(n_cent):
            total = total + jnp.exp(norms[r, d] - top)
        norm = top + jnp.log(total)
        if r == ROUNDS - 1:
            norm_ref[...] = norm
        factor[...] = weight_ref[...] * jnp.exp(peaks[...] - norm)

        partial[...] = jnp.zeros_like(partial)

        def gather(i, _):
            cols = pl.ds(pl.multiple_of(i * TILE2, TILE2), TILE2)
            f = jnp.concatenate(
                [factor[pl.ds(i * (TILE2 // LANES) + j, 1), :] for j in range(TILE2 // LANES)], axis=1
            )
            g1, g2 = split(embed_ref[:, cols] * f)
            f1, f2 = split(jnp.broadcast_to(f, (features, TILE2)))
            scaled = jnp.concatenate([g1, g2.astype(BF16), f1, f2.astype(BF16)], axis=0)
            dims = (((1,), (1,)), ((), ()))
            partial[...] += lax.dot_general(
                high[:, cols], scaled, dims, preferred_element_type=F32
            ) + lax.dot_general(low[:, cols], scaled, dims, preferred_element_type=F32)
            return 0

        lax.fori_loop(0, cells // TILE2, gather, 0)

        moment = partial[:, :LANES]
        moment = moment + pltpu.roll(moment, features, 1)
        mass = partial[:, LANES:]
        mass = mass + pltpu.roll(mass, features, 1)
        partial[:, :LANES] = jnp.where(left, moment, mass)

        copies = []
        for d in range(1, n_cells):
            peer = lax.rem(me_cells + d, n_cells)
            copy = pltpu.make_async_remote_copy(
                src_ref=partial.at[pl.ds(pl.multiple_of(peer * chunk, chunk), chunk), pl.ds(0, LANES)],
                dst_ref=parts.at[r, d],
                send_sem=part_send.at[r, d],
                recv_sem=part_recv.at[r, d],
                device_id={"cells": peer},
                device_id_type=MESH,
            )
            copy.start()
            copies.append(copy)
        mine = pl.ds(pl.multiple_of(me_cells * chunk, chunk), chunk)
        total = partial[mine, pl.ds(0, LANES)]
        for copy in copies:
            copy.wait()
        for d in range(1, n_cells):
            total = total + parts[r, d]
        fresh = (total + PRIOR * current[r, mine, :]) / (pltpu.roll(total, features, 1) + PRIOR)
        current[r + 1, mine, :] = jnp.where(
            lax.broadcasted_iota(jnp.int32, (chunk, LANES), 1) < features,
            fresh,
            pltpu.roll(fresh, features, 1),
        )
        copies = []
        for d in range(1, n_cells):
            copy = pltpu.make_async_remote_copy(
                src_ref=current.at[r + 1, mine],
                dst_ref=current.at[r + 1, mine],
                send_sem=new_send.at[r, d],
                recv_sem=new_recv.at[r, d],
                device_id={"cells": lax.rem(me_cells + d, n_cells)},
                device_id_type=MESH,
            )
            copy.start()
            copies.append(copy)
        for copy in copies:
            copy.wait()

    out_ref[...] = current[ROUNDS].T[:features, :]


def on_device(embed, centroids, cell_weight):
    n_cells = lax.axis_size("cells")
    n_cent = lax.axis_size("cent")
    features, cells = embed.shape
    width = centroids.shape[1]
    rows = cells // LANES
    vmem = pl.BlockSpec(memory_space=pltpu.VMEM)
    dma = pltpu.SemaphoreType.DMA
    current, norms = pl.pallas_call(
        functools.partial(kernel, n_cells, n_cent),
        out_shape=(
            jax.ShapeDtypeStruct((features, width), F32),
            jax.ShapeDtypeStruct((rows, LANES), F32),
        ),
        in_specs=[vmem] * 3,
        out_specs=(vmem, vmem),
        scratch_shapes=[
            pltpu.VMEM((8 * features, cells), BF16),
            pltpu.VMEM((width, 4 * LANES), BF16),
            pltpu.VMEM((width, cells), BF16),
            pltpu.VMEM((width, cells), BF16),
            pltpu.VMEM((width, TILE), F32),
            pltpu.VMEM((rows, LANES), F32),
            pltpu.VMEM((rows, LANES), F32),
            pltpu.VMEM((rows, LANES), F32),
            pltpu.VMEM((ROUNDS + 1, width, LANES), F32),
            pltpu.VMEM((width, 2 * LANES), F32),
            pltpu.VMEM((ROUNDS, n_cent, rows, LANES), F32),
            pltpu.VMEM((ROUNDS, n_cells, width // n_cells, LANES), F32),
            dma((ROUNDS, n_cent)),
            dma((ROUNDS, n_cent)),
            dma((ROUNDS, n_cells)),
            dma((ROUNDS, n_cells)),
            dma((ROUNDS, n_cells)),
            dma((ROUNDS, n_cells)),
        ],
        compiler_params=pltpu.CompilerParams(
            collective_id=0, has_side_effects=True, vmem_limit_bytes=56 * 1024 * 1024
        ),
    )(embed, centroids, cell_weight.reshape(rows, LANES))
    return (current, norms.reshape(cells))


def solution(mesh):
    in_specs = (P(None, "cells"), P(None, "cent"), P("cells"))
    out_specs = (P(None, "cent"), P("cells"))
    return jax.shard_map(
        on_device, mesh=mesh, in_specs=in_specs, out_specs=out_specs, check_vma=False
    )
```

```python
import functools

import jax
import jax.numpy as jnp
from jax import lax
from jax.experimental import pallas as pl
from jax.experimental.pallas import tpu as pltpu
from jax.sharding import PartitionSpec as P

ROUNDS = 2
INV_TEMP = 0.125
PRIOR = 1.0
TILE = 256
TILE2 = 1024
HALVES = 2
LANES = 128
MESH = pl.DeviceIdType.MESH
BF16 = jnp.bfloat16
F32 = jnp.float32


def split(x):
    high = x.astype(BF16)
    return high, x - high.astype(F32)


def kernel(
    n_cells, n_cent,
    embed_ref, cent_ref, weight_ref,
    out_ref, norm_ref,
    points, table, high, low, logits, peaks, sums, factor,
    packed, partial, outgoing, norms, parts,
    norm_send, norm_recv, part_send, part_recv, new_send, new_recv,
):
    features, cells = embed_ref.shape
    width = cent_ref.shape[1]
    rows = cells // LANES
    chunk = width // n_cells
    half = rows // HALVES
    tiles = cells // TILE // HALVES
    tiles2 = cells // TILE2 // HALVES
    me_cells = lax.axis_index("cells")
    me_cent = lax.axis_index("cent")

    barrier = pltpu.get_barrier_semaphore()
    for d in range(1, n_cent):
        pl.semaphore_signal(
            barrier, inc=1, device_id={"cent": lax.rem(me_cent + d, n_cent)}, device_id_type=MESH
        )
    for d in range(1, n_cells):
        pl.semaphore_signal(
            barrier, inc=1, device_id={"cells": lax.rem(me_cells + d, n_cells)}, device_id_type=MESH
        )

    def stack_points(i, _):
        cols = pl.ds(pl.multiple_of(i * TILE, TILE), TILE)
        e1, rest = split(embed_ref[:, cols])
        e2, rest = split(rest)
        e3 = rest.astype(BF16)
        for j, term in enumerate((e1, e1, e2, e2, e1, e3)):
            points[j * features:(j + 1) * features, cols] = term
        points[6 * features:, cols] = jnp.ones((2 * features, TILE), BF16)
        return 0

    lax.fori_loop(0, cells // TILE, stack_points, 0)

    lane = lax.broadcasted_iota(jnp.int32, (width, LANES), 1)
    row = lax.broadcasted_iota(jnp.int32, (width, LANES), 0)
    left = lane < features
    pair = chunk // 2
    left_pair = lax.broadcasted_iota(jnp.int32, (n_cells, pair, LANES), 2) < features

    def pack(x):
        x = x.reshape(n_cells, 2, pair, LANES)
        return jnp.where(left_pair, x[:, 0], x[:, 1])

    def unpack(x):
        other = pltpu.roll(x, features, 2)
        low_rows = jnp.where(left_pair, x, other)
        high_rows = jnp.where(left_pair, other, x)
        return jnp.stack([low_rows, high_rows], axis=1).reshape(width, LANES)

    start = cent_ref[...].T
    both = jnp.concatenate([start, start], axis=1)
    packed[0] = pack(both)

    for r in range(ROUNDS):
        half_square = 0.5 * jnp.sum(jnp.where(left, both * both, 0.0), axis=1, keepdims=True)
        c1, rest = split(both * INV_TEMP)
        c2, rest = split(rest)
        c3 = rest
        h1, rest = split(jnp.broadcast_to(half_square * -INV_TEMP, (width, LANES)))
        h2, h3 = split(rest)
        c1, c2, h1, h2 = (x.astype(F32) for x in (c1, c2, h1, h2))
        first = jnp.where(left, c1, c2).astype(BF16)
        table[:, 0:LANES] = first
        table[:, LANES:2 * LANES] = first
        table[:, 2 * LANES:3 * LANES] = jnp.where(left, c3, c1).astype(BF16)
        table[:, 3 * LANES:] = jnp.where(
            lane == 0, h1, jnp.where(lane == 1, h2, jnp.where(lane == 2, h3, 0.0))
        ).astype(BF16)

        def score(i, _):
            cols = pl.ds(pl.multiple_of(i * TILE, TILE), TILE)
            logits[...] = jnp.dot(table[...], points[:, cols], preferred_element_type=F32)
            step = 64
            peak = logits[0:step, :]
            for k in range(step, width, step):
                peak = jnp.maximum(peak, logits[k:k + step, :])
            peak = jnp.max(peak, axis=0, keepdims=True)
            total = jnp.zeros((step, TILE), F32)
            for k in range(0, width, step):
                p = jnp.exp(logits[k:k + step, :] - peak)
                total = total + p
                p1, p2 = split(p)
                high[k:k + step, cols] = p1
                low[k:k + step, cols] = p2.astype(BF16)
            total = jnp.sum(total, axis=0, keepdims=True)
            for j in range(TILE // LANES):
                row = pl.ds(i * (TILE // LANES) + j, 1)
                peaks[row, :] = peak[:, j * LANES:(j + 1) * LANES]
                sums[row, :] = total[:, j * LANES:(j + 1) * LANES]
            return 0

        pending = []
        for h in range(HALVES):
            lax.fori_loop(h * tiles, (h + 1) * tiles, score, 0)
            span = pl.ds(h * half, half)
            norms[r, me_cent, span] = peaks[span] + jnp.log(sums[span])
            if r == 0 and h == 0:
                pl.semaphore_wait(barrier, n_cent + n_cells - 2)
            copies = []
            for d in range(1, n_cent):
                copy = pltpu.make_async_remote_copy(
                    src_ref=norms.at[r, me_cent, span],
                    dst_ref=norms.at[r, me_cent, span],
                    send_sem=norm_send.at[r, h, d],
                    recv_sem=norm_recv.at[r, h, d],
                    device_id={"cent": lax.rem(me_cent + d, n_cent)},
                    device_id_type=MESH,
                )
                copy.start()
                copies.append(copy)
            pending.append(copies)

        partial[...] = jnp.zeros_like(partial)

        def gather(i, _):
            cols = pl.ds(pl.multiple_of(i * TILE2, TILE2), TILE2)
            f = jnp.concatenate(
                [factor[pl.ds(i * (TILE2 // LANES) + j, 1), :] for j in range(TILE2 // LANES)], axis=1
            )
            g1, g2 = split(embed_ref[:, cols] * f)
            f1, f2 = split(jnp.broadcast_to(f, (features, TILE2)))
            scaled = jnp.concatenate([g1, g2.astype(BF16), f1, f2.astype(BF16)], axis=0)
            dims = (((1,), (1,)), ((), ()))
            partial[...] += lax.dot_general(
                high[:, cols], scaled, dims, preferred_element_type=F32
            ) + lax.dot_general(low[:, cols], scaled, dims, preferred_element_type=F32)
            return 0

        for h in range(HALVES):
            for copy in pending[h]:
                copy.wait()
            span = pl.ds(h * half, half)
            top = norms[r, 0, span]
            for d in range(1, n_cent):
                top = jnp.maximum(top, norms[r, d, span])
            total = jnp.zeros((half, LANES), F32)
            for d in range(n_cent):
                total = total + jnp.exp(norms[r, d, span] - top)
            norm = top + jnp.log(total)
            if r == ROUNDS - 1:
                norm_ref[span] = norm
            factor[span] = weight_ref[span] * jnp.exp(peaks[span] - norm)
            lax.fori_loop(h * tiles2, (h + 1) * tiles2, gather, 0)

        moment = partial[:, :LANES]
        moment = moment + pltpu.roll(moment, features, 1)
        mass = partial[:, LANES:]
        mass = mass + pltpu.roll(mass, features, 1)
        outgoing[:, :pair] = pack(moment)
        mass = jnp.where(lane == lax.rem(row, chunk), mass, 0.0)
        mass = jnp.sum(mass.reshape(n_cells, chunk, LANES), axis=1, keepdims=True)
        outgoing[:, pair:] = jnp.broadcast_to(mass, (n_cells, 8, LANES))

        copies = []
        for d in range(1, n_cells):
            peer = lax.rem(me_cells + d, n_cells)
            copy = pltpu.make_async_remote_copy(
                src_ref=outgoing.at[peer],
                dst_ref=parts.at[r, d],
                send_sem=part_send.at[r, d],
                recv_sem=part_recv.at[r, d],
                device_id={"cells": peer},
                device_id_type=MESH,
            )
            copy.start()
            copies.append(copy)
        total = outgoing[me_cells]
        for d in range(1, n_cells):
            copies[d - 1].wait()
            total = total + parts[r, d]
        mass = jnp.broadcast_to(total[pair:pair + 1], (pair, LANES))
        lane_p = lax.broadcasted_iota(jnp.int32, (pair, LANES), 1)
        row_p = lax.broadcasted_iota(jnp.int32, (pair, LANES), 0)
        mass_l = jnp.sum(jnp.where(lane_p == row_p, mass, 0.0), axis=1, keepdims=True)
        mass_r = jnp.sum(jnp.where(lane_p == row_p + pair, mass, 0.0), axis=1, keepdims=True)
        mass = jnp.where(lane_p < features, mass_l, mass_r)
        packed[r + 1, me_cells] = (total[:pair] + PRIOR * packed[r, me_cells]) / (mass + PRIOR)
        copies = []
        for d in range(1, n_cells):
            copy = pltpu.make_async_remote_copy(
                src_ref=packed.at[r + 1, me_cells],
                dst_ref=packed.at[r + 1, me_cells],
                send_sem=new_send.at[r, d],
                recv_sem=new_recv.at[r, d],
                device_id={"cells": lax.rem(me_cells + d, n_cells)},
                device_id_type=MESH,
            )
            copy.start()
            copies.append(copy)
        for copy in copies:
            copy.wait()
        both = unpack(packed[r + 1])

    out_ref[...] = both.T[:features, :]


def on_device(embed, centroids, cell_weight):
    n_cells = lax.axis_size("cells")
    n_cent = lax.axis_size("cent")
    features, cells = embed.shape
    width = centroids.shape[1]
    rows = cells // LANES
    pair = width // n_cells // 2
    vmem = pl.BlockSpec(memory_space=pltpu.VMEM)
    dma = pltpu.SemaphoreType.DMA
    current, norms = pl.pallas_call(
        functools.partial(kernel, n_cells, n_cent),
        out_shape=(
            jax.ShapeDtypeStruct((features, width), F32),
            jax.ShapeDtypeStruct((rows, LANES), F32),
        ),
        in_specs=[vmem] * 3,
        out_specs=(vmem, vmem),
        scratch_shapes=[
            pltpu.VMEM((8 * features, cells), BF16),
            pltpu.VMEM((width, 4 * LANES), BF16),
            pltpu.VMEM((width, cells), BF16),
            pltpu.VMEM((width, cells), BF16),
            pltpu.VMEM((width, TILE), F32),
            pltpu.VMEM((rows, LANES), F32),
            pltpu.VMEM((rows, LANES), F32),
            pltpu.VMEM((rows, LANES), F32),
            pltpu.VMEM((ROUNDS + 1, n_cells, pair, LANES), F32),
            pltpu.VMEM((width, 2 * LANES), F32),
            pltpu.VMEM((n_cells, pair + 8, LANES), F32),
            pltpu.VMEM((ROUNDS, n_cent, rows, LANES), F32),
            pltpu.VMEM((ROUNDS, n_cells, pair + 8, LANES), F32),
            dma((ROUNDS, HALVES, n_cent)),
            dma((ROUNDS, HALVES, n_cent)),
            dma((ROUNDS, n_cells)),
            dma((ROUNDS, n_cells)),
            dma((ROUNDS, n_cells)),
            dma((ROUNDS, n_cells)),
        ],
        compiler_params=pltpu.CompilerParams(
            collective_id=0, has_side_effects=True, vmem_limit_bytes=56 * 1024 * 1024
        ),
    )(embed, centroids, cell_weight.reshape(rows, LANES))
    return (current, norms.reshape(cells))


def solution(mesh):
    in_specs = (P(None, "cells"), P(None, "cent"), P("cells"))
    out_specs = (P(None, "cent"), P("cells"))
    return jax.shard_map(
        on_device, mesh=mesh, in_specs=in_specs, out_specs=out_specs, check_vma=False
    )
```

```python
import functools

import jax
import jax.numpy as jnp
from jax import lax
from jax.experimental import pallas as pl
from jax.experimental.pallas import tpu as pltpu
from jax.sharding import PartitionSpec as P

ROUNDS = 2
INV_TEMP = 0.125
PRIOR = 1.0
TILE = 256
HALVES = 2
LANES = 128
MESH = pl.DeviceIdType.MESH
BF16 = jnp.bfloat16
F32 = jnp.float32


def split(x):
    high = x.astype(BF16)
    return high, x - high.astype(F32)


def kernel(
    n_cells, n_cent, blocks,
    embed_ref, cent_ref, weight_ref,
    out_ref, norm_ref,
    points, table, high, low, logits_a, logits_b, peaks, sums, factor,
    packed, partial, outgoing, norms, parts,
    norm_send, norm_recv, part_send, part_recv, new_send, new_recv,
):
    features, cells = embed_ref.shape
    width = cent_ref.shape[1] // blocks
    rows = cells // LANES
    chunk = width // n_cells
    pair = chunk // 2
    half = rows // HALVES
    half_cells = cells // HALVES
    tiles = cells // TILE // HALVES
    me_cells = lax.axis_index("cells")
    me_cent = lax.axis_index("cent")

    barrier = pltpu.get_barrier_semaphore()
    for d in range(1, n_cent):
        pl.semaphore_signal(
            barrier, inc=1, device_id={"cent": lax.rem(me_cent + d, n_cent)}, device_id_type=MESH
        )
    for d in range(1, n_cells):
        pl.semaphore_signal(
            barrier, inc=1, device_id={"cells": lax.rem(me_cells + d, n_cells)}, device_id_type=MESH
        )

    def stack_points(i, _):
        cols = pl.ds(pl.multiple_of(i * TILE, TILE), TILE)
        e1, rest = split(embed_ref[:, cols])
        e2, rest = split(rest)
        e3 = rest.astype(BF16)
        for j, term in enumerate((e1, e1, e2, e2, e1, e3)):
            points[j * features:(j + 1) * features, cols] = term
        points[6 * features:, cols] = jnp.ones((2 * features, TILE), BF16)
        return 0

    lax.fori_loop(0, cells // TILE, stack_points, 0)

    lane = lax.broadcasted_iota(jnp.int32, (width, LANES), 1)
    row = lax.broadcasted_iota(jnp.int32, (width, LANES), 0)
    left = lane < features
    left_pair = lax.broadcasted_iota(jnp.int32, (n_cells, pair, LANES), 2) < features

    def pack(x):
        x = x.reshape(n_cells, 2, pair, LANES)
        return jnp.where(left_pair, x[:, 0], x[:, 1])

    def unpack(x):
        other = pltpu.roll(x, features, 2)
        low_rows = jnp.where(left_pair, x, other)
        high_rows = jnp.where(left_pair, other, x)
        return jnp.stack([low_rows, high_rows], axis=1).reshape(width, LANES)

    def load_block(r, b):
        if r == 0:
            start = cent_ref[:, b * width:(b + 1) * width].T
            both = jnp.concatenate([start, start], axis=1)
            packed[0, b] = pack(both)
            return both
        for copy in arriving[b]:
            copy.wait()
        return unpack(packed[r, b])

    def fill_table(b, both):
        out = slice(b * width, (b + 1) * width)
        half_square = 0.5 * jnp.sum(jnp.where(left, both * both, 0.0), axis=1, keepdims=True)
        c1, rest = split(both * INV_TEMP)
        c2, rest = split(rest)
        c3 = rest
        h1, rest = split(jnp.broadcast_to(half_square * -INV_TEMP, (width, LANES)))
        h2, h3 = split(rest)
        c1, c2, h1, h2 = (x.astype(F32) for x in (c1, c2, h1, h2))
        first = jnp.where(left, c1, c2).astype(BF16)
        table[out, 0:LANES] = first
        table[out, LANES:2 * LANES] = first
        table[out, 2 * LANES:3 * LANES] = jnp.where(left, c3, c1).astype(BF16)
        table[out, 3 * LANES:] = jnp.where(
            lane == 0, h1, jnp.where(lane == 1, h2, jnp.where(lane == 2, h3, 0.0))
        ).astype(BF16)

    def score(b, h):
        base = b * width

        def columns(i):
            return pl.ds(pl.multiple_of(i * TILE, TILE), TILE)

        def product(buffer, i):
            buffer[...] = jnp.dot(
                table[base:base + width, :], points[:, columns(i)], preferred_element_type=F32
            )

        def weigh(buffer, i):
            cols = columns(i)
            step = 64
            peak = buffer[0:step, :]
            for k in range(step, width, step):
                peak = jnp.maximum(peak, buffer[k:k + step, :])
            peak = jnp.max(peak, axis=0, keepdims=True)
            total = jnp.zeros((step, TILE), F32)
            for k in range(0, width, step):
                p = jnp.exp(buffer[k:k + step, :] - peak)
                total = total + p
                p1, p2 = split(p)
                high[base + k:base + k + step, cols] = p1
                low[base + k:base + k + step, cols] = p2.astype(BF16)
            total = jnp.sum(total, axis=0, keepdims=True)
            for j in range(TILE // LANES):
                at = pl.ds(i * (TILE // LANES) + j, 1)
                peaks[b, at, :] = peak[:, j * LANES:(j + 1) * LANES]
                sums[b, at, :] = total[:, j * LANES:(j + 1) * LANES]

        first = h * tiles

        def step_pair(i, _):
            at = first + 2 * i
            product(logits_b, at + 1)
            weigh(logits_a, at)
            product(logits_a, at + 2)
            weigh(logits_b, at + 1)
            return 0

        product(logits_a, first)
        lax.fori_loop(0, tiles // 2 - 1, step_pair, 0)
        product(logits_b, first + tiles - 1)
        weigh(logits_a, first + tiles - 2)
        weigh(logits_b, first + tiles - 1)

    def send_norms(r, h):
        span = pl.ds(h * half, half)
        top = peaks[0, span]
        for b in range(1, blocks):
            top = jnp.maximum(top, peaks[b, span])
        total = jnp.zeros((half, LANES), F32)
        for b in range(blocks):
            total = total + sums[b, span] * jnp.exp(peaks[b, span] - top)
        norms[r, me_cent, span] = top + jnp.log(total)
        if r == 0 and h == 0:
            pl.semaphore_wait(barrier, n_cent + n_cells - 2)
        copies = []
        for d in range(1, n_cent):
            copy = pltpu.make_async_remote_copy(
                src_ref=norms.at[r, me_cent, span],
                dst_ref=norms.at[r, me_cent, span],
                send_sem=norm_send.at[r, h, d],
                recv_sem=norm_recv.at[r, h, d],
                device_id={"cent": lax.rem(me_cent + d, n_cent)},
                device_id_type=MESH,
            )
            copy.start()
            copies.append(copy)
        return copies

    def take_norms(r, h, copies):
        for copy in copies:
            copy.wait()
        span = pl.ds(h * half, half)
        top = norms[r, 0, span]
        for d in range(1, n_cent):
            top = jnp.maximum(top, norms[r, d, span])
        total = jnp.zeros((half, LANES), F32)
        for d in range(n_cent):
            total = total + jnp.exp(norms[r, d, span] - top)
        norm = top + jnp.log(total)
        if r == ROUNDS - 1:
            norm_ref[span] = norm
        for b in range(blocks):
            factor[b, span] = weight_ref[span] * jnp.exp(peaks[b, span] - norm)

    def gather(b, h):
        cols = pl.ds(h * half_cells, half_cells)
        out = slice(b * width, (b + 1) * width)
        f = jnp.concatenate([factor[b, h * half + j:h * half + j + 1, :] for j in range(half)], axis=1)
        g1, g2 = split(embed_ref[:, cols] * f)
        f1, f2 = split(jnp.broadcast_to(f, (features, half_cells)))
        scaled = jnp.concatenate([g1, g2.astype(BF16), f1, f2.astype(BF16)], axis=0)
        dims = (((1,), (1,)), ((), ()))
        sums_now = lax.dot_general(
            high[out, cols], scaled, dims, preferred_element_type=F32
        ) + lax.dot_general(low[out, cols], scaled, dims, preferred_element_type=F32)
        if h == 0:
            partial[...] = sums_now
        else:
            partial[...] += sums_now

    def send_parts(r, b):
        moment = partial[:, :LANES]
        moment = moment + pltpu.roll(moment, features, 1)
        mass = partial[:, LANES:]
        mass = mass + pltpu.roll(mass, features, 1)
        outgoing[r, b, :, :pair] = pack(moment)
        mass = jnp.where(lane == lax.rem(row, chunk), mass, 0.0)
        mass = jnp.sum(mass.reshape(n_cells, chunk, LANES), axis=1, keepdims=True)
        outgoing[r, b, :, pair:] = jnp.broadcast_to(mass, (n_cells, 8, LANES))
        copies = []
        for d in range(1, n_cells):
            peer = lax.rem(me_cells + d, n_cells)
            copy = pltpu.make_async_remote_copy(
                src_ref=outgoing.at[r, b, peer],
                dst_ref=parts.at[r, b, d],
                send_sem=part_send.at[r, b, d],
                recv_sem=part_recv.at[r, b, d],
                device_id={"cells": peer},
                device_id_type=MESH,
            )
            copy.start()
            copies.append(copy)
        return copies

    def send_new(r, b, copies):
        total = outgoing[r, b, me_cells]
        for d in range(1, n_cells):
            copies[d - 1].wait()
            total = total + parts[r, b, d]
        mass = jnp.broadcast_to(total[pair:pair + 1], (pair, LANES))
        lane_p = lax.broadcasted_iota(jnp.int32, (pair, LANES), 1)
        row_p = lax.broadcasted_iota(jnp.int32, (pair, LANES), 0)
        mass_l = jnp.sum(jnp.where(lane_p == row_p, mass, 0.0), axis=1, keepdims=True)
        mass_r = jnp.sum(jnp.where(lane_p == row_p + pair, mass, 0.0), axis=1, keepdims=True)
        mass = jnp.where(lane_p < features, mass_l, mass_r)
        packed[r + 1, b, me_cells] = (total[:pair] + PRIOR * packed[r, b, me_cells]) / (mass + PRIOR)
        copies = []
        for d in range(1, n_cells):
            copy = pltpu.make_async_remote_copy(
                src_ref=packed.at[r + 1, b, me_cells],
                dst_ref=packed.at[r + 1, b, me_cells],
                send_sem=new_send.at[r, b, d],
                recv_sem=new_recv.at[r, b, d],
                device_id={"cells": lax.rem(me_cells + d, n_cells)},
                device_id_type=MESH,
            )
            copy.start()
            copies.append(copy)
        return copies

    arriving = []
    for r in range(ROUNDS):
        pending = []
        for b in range(blocks):
            fill_table(b, load_block(r, b))
            for h in range(HALVES):
                score(b, h)
                if b == blocks - 1:
                    pending.append(send_norms(r, h))
        leaving = []
        for b in range(blocks):
            for h in range(HALVES):
                if b == 0:
                    take_norms(r, h, pending[h])
                gather(b, h)
            leaving.append(send_parts(r, b))
        arriving = [send_new(r, b, leaving[b]) for b in range(blocks)]
    for b in range(blocks):
        both = load_block(ROUNDS, b)
        out_ref[:, b * width:(b + 1) * width] = both.T[:features, :]


def hand_over(current_ref, norm_ref, out_ref, norm_out_ref):
    out_ref[...] = current_ref[...]
    norm_out_ref[...] = norm_ref[...]


def on_device(embed, centroids, cell_weight):
    n_cells = lax.axis_size("cells")
    n_cent = lax.axis_size("cent")
    features, cells = embed.shape
    width = centroids.shape[1]
    rows = cells // LANES
    blocks = 1
    block = width // blocks
    pair = block // n_cells // 2
    vmem = pl.BlockSpec(memory_space=pltpu.VMEM)
    dma = pltpu.SemaphoreType.DMA
    current, norms = pl.pallas_call(
        functools.partial(kernel, n_cells, n_cent, blocks),
        out_shape=(
            jax.ShapeDtypeStruct((features, width), F32),
            jax.ShapeDtypeStruct((rows, LANES), F32),
        ),
        in_specs=[vmem] * 3,
        out_specs=(vmem, vmem),
        scratch_shapes=[
            pltpu.VMEM((8 * features, cells), BF16),
            pltpu.VMEM((width, 4 * LANES), BF16),
            pltpu.VMEM((width, cells), BF16),
            pltpu.VMEM((width, cells), BF16),
            pltpu.VMEM((block, TILE), F32),
            pltpu.VMEM((block, TILE), F32),
            pltpu.VMEM((blocks, rows, LANES), F32),
            pltpu.VMEM((blocks, rows, LANES), F32),
            pltpu.VMEM((blocks, rows, LANES), F32),
            pltpu.VMEM((ROUNDS + 1, blocks, n_cells, pair, LANES), F32),
            pltpu.VMEM((block, 2 * LANES), F32),
            pltpu.VMEM((ROUNDS, blocks, n_cells, pair + 8, LANES), F32),
            pltpu.VMEM((ROUNDS, n_cent, rows, LANES), F32),
            pltpu.VMEM((ROUNDS, blocks, n_cells, pair + 8, LANES), F32),
            dma((ROUNDS, HALVES, n_cent)),
            dma((ROUNDS, HALVES, n_cent)),
            dma((ROUNDS, blocks, n_cells)),
            dma((ROUNDS, blocks, n_cells)),
            dma((ROUNDS, blocks, n_cells)),
            dma((ROUNDS, blocks, n_cells)),
        ],
        compiler_params=pltpu.CompilerParams(
            collective_id=0, has_side_effects=True, vmem_limit_bytes=56 * 1024 * 1024
        ),
    )(embed, centroids, cell_weight.reshape(rows, LANES))
    current, norms = pl.pallas_call(
        hand_over,
        out_shape=(
            jax.ShapeDtypeStruct((features, width), F32),
            jax.ShapeDtypeStruct((rows, LANES), F32),
        ),
        in_specs=[vmem] * 2,
        out_specs=(vmem, vmem),
    )(current, norms)
    return (current, norms.reshape(cells))


def solution(mesh):
    in_specs = (P(None, "cells"), P(None, "cent"), P("cells"))
    out_specs = (P(None, "cent"), P("cells"))
    return jax.shard_map(
        on_device, mesh=mesh, in_specs=in_specs, out_specs=out_specs, check_vma=False
    )
```
